128 devices in a mesh: tx: 16 (over z, x), ty: 8 (over y, core).
Axes of the slice: x: 4, y: 4, z: 4, core: 2. Of those that a mesh axis runs over, the one named last changes fastest.
Arguments:
- sar_image: bfloat16 [2, 8192, 512], P(None, ('tx', 'ty')), may hold values from -6 to 6
- kernel_first: bfloat16 [16, 2, 3, 3], replicated, may hold values from -2 to 2
- kernel_second: bfloat16 [16, 16, 3, 3], replicated, may hold values from -0.75 to 0.75
- kernel_third: bfloat16 [16, 16, 3, 3], replicated, may hold values from -0.75 to 0.75
- kernel_last: bfloat16 [1, 16, 3, 3], replicated, may hold values from -1 to 1
- geo_weight: float32 [8192, 512], P(('tx', 'ty')), may hold values from 0.25 to 1
- cell_index: int32 [8192, 512], P(('tx', 'ty')), may hold values from 0 to 511
- block_tile: int32 [8192, 1], P(('tx', 'ty')), may hold values from 0 to 127; in each aligned block of 64 rows (0 to 63, 64 to 127, ...) at most 2 rows name the same one
- block_row: int32 [8192, 1], P(('tx', 'ty')), may hold values from 0 to 254
- depth: float32 [4096, 2048], P('tx', 'ty'), may hold values from 0.1 to 1
- slope: float32 [4096, 2048], P('tx', 'ty'), may hold values from 0.01 to 1
- flow_dir: int32 [4096, 2048], P('tx', 'ty'), may hold values from 0 to 7
- rain: float32 [4096, 2048], P('tx', 'ty'), may hold values from 0 to 0.1
Outputs:
- water_fraction: bfloat16 [8192, 512], P(('tx', 'ty'))
- level: float32 [4096, 2048], P('tx', 'ty')
The draws below stay inside these ranges and needn't reach their ends.
Inputs may be any that keep to these rules, and one draw needn't show every extreme that they name: `block_tile`: in the rows of one device no tile is named more than 2 times, a bound that some block reaches.
All inputs are finite; a program needn't handle non-finite values.
Results may differ from the reference program's by a relative error of at most 0.003.
The reference program's roundings to bfloat16 on the way count: a program that leaves them out, or rounds other values in their place, can miss the bound.
Values may be sent and summed in bfloat16 or wider, within the bound.
A program may use at most 128 MiB of HBM per device.

```python
import math
import jax
import jax.numpy as jnp
import numpy as np
from jax import lax

POLAR = 2
CHANNELS = 16
AZ_DEV = 64
RANGE_PX = 512
TILE_ROWS = 256
TILE_COLS = 256
WIN_ROWS = 2
SUBSTEPS = 8
AZ_ROWS = 8192
WIN_CELLS = 512
CAPACITY = 2
MAP_ROWS = 4096
MAP_COLS = 2048
N_TY = 8
DEVICES = 128


def place_ends(entries, own_key, least, largest):
    spot = [jax.random.randint(jax.random.fold_in(own_key, axis), (), 0, length) for axis, length in enumerate(entries.shape)]
    widest = entries.shape.index(max(entries.shape))
    neighbour = spot[:widest] + [(spot[widest] + 1) % entries.shape[widest]] + spot[widest + 1:]
    return entries.at[tuple(spot)].set(least).at[tuple(neighbour)].set(largest)


def block_levels(own_key, dims, split, low, top_value):
    factor_of = 1.0
    for dim, parts in split:
        draws = jax.random.uniform(jax.random.fold_in(jax.random.fold_in(own_key, 6), dim), (parts,), jnp.float32, low / len(split), top_value / len(split))
        factor_of = factor_of * jnp.repeat(jnp.exp(draws), dims[dim] // parts).reshape((-1,) + (1,) * (len(dims) - 1 - dim))
    return factor_of


def assign_block(rng, own, number, rows, amount, top, bound, skew):
    order = jax.random.permutation(rng, amount)
    packed, ordinary = load_shares(amount, rows * top, bound, skew, True), load_shares(amount, rows * top, bound, skew, False)
    places = jnp.arange(amount)

    def named(sizes, turn):
        used = int((sizes > 0).sum())
        fixed = max(1, used // 4)
        shifted = fixed + (places - fixed + turn * (used - fixed)) % max(1, amount - fixed)
        return jnp.zeros((amount,), jnp.int32).at[order[jnp.where(places < fixed, places, shifted)]].set(jnp.asarray(sizes, jnp.int32))

    sizes = jnp.where(number % 4 == 0, named(packed, number // 4), named(ordinary, number - number // 4 - 1))
    mixed = jax.random.permutation(jax.random.fold_in(own, 3), amount)
    donor, sink = mixed[0:amount // 2 * 2:2], mixed[1:amount // 2 * 2:2]
    room = jnp.minimum(sizes[donor] - 1, bound - sizes[sink]) // 2
    room = jnp.where((donor == order[0]) | (sink == order[0]) | (sizes[sink] == 0), 0, jnp.maximum(room, 0))
    shifted = jax.random.randint(jax.random.fold_in(own, 4), (amount // 2,), 0, 1 << 20) % (room + 1)
    sizes = sizes.at[donor].add(-shifted).at[sink].add(shifted)
    items = jnp.searchsorted(jnp.cumsum(sizes), jnp.arange(rows * top), side="right").astype(jnp.int32)
    listing = items.reshape(top, rows).T
    listing = listing[jax.random.permutation(jax.random.fold_in(own, 1), rows)]
    turn = jax.random.randint(jax.random.fold_in(own, 2), (rows, 1), 0, top)
    return jnp.take_along_axis(listing, (jnp.arange(top)[None, :] + turn) % top, axis=1)


def load_shares(count, total, limit, skew, full):
    weights = [(1 << 20) // math.isqrt(rank ** skew) + 1 for rank in range(1, count + 1)]
    largest = limit if full else min(limit, max(-(-total // count), total * weights[0] // sum(weights)))
    least = 1 if total - largest >= count - 1 else 0
    holding, surplus = [largest] + [least] * (count - 1), total - largest - least * (count - 1)
    while surplus > 0:
        movable = [i for i in range(1, count) if holding[i] < largest] or [i for i in range(1, count) if holding[i] < limit]
        mass, budget = sum([weights[i] for i in movable]), surplus
        for i in movable:
            addition = min(limit - holding[i], max(1, budget * weights[i] // mass), surplus)
            holding[i] = holding[i] + addition
            surplus = surplus - addition
    return np.array(holding)


def centred(stream_key, shape, spread, most, shards=(), kind=jnp.bfloat16):
    drawn = spread * jax.random.normal(stream_key, shape, jnp.float32)
    if shards:
        drawn = drawn * block_levels(stream_key, shape, shards, -0.22, 0.18)
    return jnp.clip(drawn, -most, most).astype(kind)


def setup_inputs(seed: int = 0) -> dict:
    seeds = jax.random.split(jax.random.key(seed), 14)
    sar_image = centred(seeds[0], (POLAR, AZ_ROWS, RANGE_PX), 1.0, 6.0, ((1, 128),))
    kernel_first = centred(seeds[1], (CHANNELS, POLAR, 3, 3), (9 * POLAR // 2) ** -0.5, 2.0)
    kernel_second = centred(seeds[2], (CHANNELS, CHANNELS, 3, 3), (9 * CHANNELS // 2) ** -0.5, 0.75)
    kernel_third = centred(seeds[3], (CHANNELS, CHANNELS, 3, 3), (9 * CHANNELS // 2) ** -0.5, 0.75)
    kernel_last = centred(seeds[4], (1, CHANNELS, 3, 3), (9 * CHANNELS // 4) ** -0.5, 1.0)
    geo_weight = jnp.clip(0.25 + 0.75 * jax.random.uniform(seeds[5], (AZ_ROWS, RANGE_PX), jnp.float32) ** block_levels(seeds[5], (AZ_ROWS, RANGE_PX), ((0, 128),), -0.2, 0.2), 0.25, 1.0)
    cell_index = place_ends(jax.random.randint(seeds[6], (AZ_ROWS, RANGE_PX), 0, WIN_CELLS), jax.random.fold_in(seeds[6], 1), 0, WIN_CELLS - 1).astype(jnp.int32)
    block_tile_keys = jax.random.split(jax.random.fold_in(seeds[7], 1), AZ_ROWS // AZ_DEV)
    block_tile_turns = jax.random.permutation(jax.random.fold_in(seeds[7], 3), AZ_ROWS // AZ_DEV)
    block_tile = jax.vmap(lambda own, number: assign_block(jax.random.fold_in(seeds[7], 2), own, number, AZ_DEV, DEVICES, 1, CAPACITY, 2))(block_tile_keys, block_tile_turns).reshape((AZ_ROWS, 1))
    block_row = place_ends(jax.random.randint(seeds[8], (AZ_ROWS, 1), 0, TILE_ROWS - WIN_ROWS + 1), jax.random.fold_in(seeds[8], 1), 0, TILE_ROWS - WIN_ROWS).astype(jnp.int32)
    depth = jnp.clip(0.1 + 0.9 * jax.random.uniform(seeds[9], (MAP_ROWS, MAP_COLS), jnp.float32) ** block_levels(seeds[9], (MAP_ROWS, MAP_COLS), ((0, 16), (1, 8)), -0.2, 0.2), 0.1, 1.0)
    slope = jnp.clip(jnp.exp(math.log(1.0) - 4.6051702 * jax.random.uniform(seeds[10], (MAP_ROWS, MAP_COLS), jnp.float32) ** block_levels(seeds[10], (MAP_ROWS, MAP_COLS), ((0, 16), (1, 8)), -0.2, 0.2)), 0.01, 1.0)
    flow_dir = place_ends(jax.random.randint(seeds[11], (MAP_ROWS, MAP_COLS), 0, 8), jax.random.fold_in(seeds[11], 1), 0, 7).astype(jnp.int32)
    rain = jnp.clip(0.1 * jax.random.uniform(seeds[12], (MAP_ROWS, MAP_COLS), jnp.float32) ** block_levels(seeds[12], (MAP_ROWS, MAP_COLS), ((0, 16), (1, 8)), -0.2, 0.2), 0.0, 0.1)
    return {"sar_image": sar_image, "kernel_first": kernel_first, "kernel_second": kernel_second, "kernel_third": kernel_third, "kernel_last": kernel_last, "geo_weight": geo_weight, "cell_index": cell_index, "block_tile": block_tile, "block_row": block_row, "depth": depth, "slope": slope, "flow_dir": flow_dir, "rain": rain}


wet_depth = 0.5
runoff_coef = 0.25
neighbour_steps = ((-1, -1), (-1, 0), (-1, 1), (0, -1), (0, 1), (1, -1), (1, 0), (1, 1))

def conv_rows(activation, kernel):
    result = lax.conv_general_dilated(activation[None], kernel, (1, 1), ((0, 0), (1, 1)), dimension_numbers=('NCHW', 'OIHW', 'NCHW'), preferred_element_type=jnp.float32)
    return result[0]

def swath_block(padded_image, start, kernels):
    activation = lax.dynamic_slice_in_dim(padded_image, start, AZ_DEV + 8, 1)
    for layer_no in range(3):
        result = conv_rows(activation, kernels[layer_no])
        rowpos = start - 4 + layer_no + 1 + jnp.arange(result.shape[1], dtype=jnp.int32)
        inside = ((rowpos >= 0) & (rowpos < AZ_ROWS)).astype(jnp.float32)
        activation = (jnp.maximum(result, 0.0) * inside[None, :, None]).astype(jnp.bfloat16)
    logit = conv_rows(activation, kernels[3])
    return jax.nn.sigmoid(logit[0]).astype(jnp.bfloat16)

def water_map(sar_image, kernels):
    padded_image = jnp.pad(sar_image, ((0, 0), (4, 4), (0, 0)))
    starts = jnp.arange(AZ_ROWS // AZ_DEV, dtype=jnp.int32) * AZ_DEV

    def one_block(start):
        return swath_block(padded_image, start, kernels)
    blocks = lax.map(one_block, starts)
    return blocks.reshape(AZ_ROWS, RANGE_PX)

def regrid(fraction, geo_weight, cell_index, block_tile, block_row):
    tile_row = block_tile[:, 0] // N_TY
    tile_col = block_tile[:, 0] % N_TY
    map_row = (tile_row * TILE_ROWS + block_row[:, 0])[:, None] + cell_index // TILE_COLS
    map_col = (tile_col * TILE_COLS)[:, None] + cell_index % TILE_COLS
    flat_ids = (map_row * MAP_COLS + map_col).reshape(-1)
    weighted = fraction.astype(jnp.float32) * geo_weight
    observed = jax.ops.segment_sum(weighted.reshape(-1), flat_ids, MAP_ROWS * MAP_COLS)
    covered = jax.ops.segment_sum(geo_weight.reshape(-1), flat_ids, MAP_ROWS * MAP_COLS)
    return (observed.reshape(MAP_ROWS, MAP_COLS), covered.reshape(MAP_ROWS, MAP_COLS))

def inflow(runoff_pad, dir_pad, extent_rows, extent_cols):
    inflow_sum = jnp.zeros((extent_rows, extent_cols), jnp.float32)
    for dir_code, (row_step, col_step) in enumerate(neighbour_steps):
        source_runoff = runoff_pad[1 - row_step:1 - row_step + extent_rows, 1 - col_step:1 - col_step + extent_cols]
        source_dir = dir_pad[1 - row_step:1 - row_step + extent_rows, 1 - col_step:1 - col_step + extent_cols]
        inflow_sum = inflow_sum + jnp.where(source_dir == dir_code, source_runoff, 0.0)
    return inflow_sum

def reference(sar_image, kernel_first, kernel_second, kernel_third, kernel_last, geo_weight, cell_index, block_tile, block_row, depth, slope, flow_dir, rain):
    kernels = (kernel_first, kernel_second, kernel_third, kernel_last)
    fraction = water_map(sar_image, kernels)
    observed, covered = regrid(fraction, geo_weight, cell_index, block_tile, block_row)
    wet = depth / (depth + wet_depth)
    innovation = (observed - covered * wet) / (covered + 1.0)
    level = depth * jnp.exp(innovation)
    conveyance = runoff_coef * jnp.sqrt(slope)
    dir_pad = jnp.pad(flow_dir, 1)
    for substep in range(SUBSTEPS):
        runoff = conveyance * level * jnp.cbrt(level) * jnp.cbrt(level)
        level = level + rain - runoff + inflow(jnp.pad(runoff, 1), dir_pad, MAP_ROWS, MAP_COLS)
    return (fraction, level)
```

```python
import functools

import jax
import jax.numpy as jnp
from jax import lax
from jax.experimental import pallas as pl
from jax.experimental.pallas import tpu as pltpu
from jax.sharding import PartitionSpec as P

F32 = jnp.float32
BF16 = jnp.bfloat16
I32 = jnp.int32

WIN_ROWS = 2
SUBSTEPS = 8
CAPACITY = 2
CHANNELS = 16
WET_DEPTH = 0.5
RUNOFF_COEF = 0.25

AZ = 64
PX = 512
HALO = 4
IMG_ROWS = 96
ROWS1 = 80
TILE = 256
DEPTH = 8
EXT_ROWS = TILE + 2 * DEPTH
EXT_COLS = TILE + 128

NN = (((1,), (0,)), ((), ()))
NT = (((1,), (1,)), ((), ()))
TN = (((0,), (0,)), ((), ()))


def dot(a, b, dims=NN):
    return lax.dot_general(a, b, dims, preferred_element_type=F32)


def iota(shape, dim):
    return lax.broadcasted_iota(I32, shape, dim)


def onehot(cond):
    return jnp.where(cond, 1.0, 0.0).astype(BF16)


def shifted(x, step):
    width = x.shape[1]
    rolled = pltpu.roll(x, step % width, 1)
    edge = 0 if step == 1 else width - 1
    return jnp.where(iota(x.shape, 1) == edge, 0.0, rolled)


def build_weights(ksmall_ref, k2_ref, k3_ref, w1_ref, w2_ref, w3_ref, w4_ref):
    spread = onehot(iota((16, 256), 1) % 16 == iota((16, 256), 0))
    band = iota((16, 256), 1) // 16
    for k_ref, w_ref in ((k2_ref, w2_ref), (k3_ref, w3_ref)):
        tiled = dot(k_ref[...], spread)
        for dx in range(3):
            taps = [tiled[(dy * 3 + dx) * 16 : (dy * 3 + dx + 1) * 16] for dy in range(3)]
            for row in range(14):
                value = jnp.zeros((16, 256), F32)
                for dy in range(3):
                    value = jnp.where(band == row + dy, taps[dy], value)
                w_ref[dx, row * 16 : (row + 1) * 16, :] = value.astype(BF16)
    lane = iota((32, 192), 1)
    taps = []
    for dy in range(3):
        source = (dy * 3 + lane // 64) * 2 + (lane // 32) % 2
        taps.append(dot(ksmall_ref[...], onehot(iota((32, 192), 0) == source), TN))
    in_row = iota((16, 192), 1) % 32
    for row in range(16):
        value = jnp.zeros((16, 192), F32)
        for dy in range(3):
            value = jnp.where(in_row == row + dy, taps[dy], value)
        w1_ref[row * 16 : (row + 1) * 16, :] = value.astype(BF16)
    tiled = dot(ksmall_ref[...], spread)
    band = iota((8, 256), 1) // 16 - iota((8, 256), 0)
    for dx in range(3):
        value = jnp.zeros((8, 256), F32)
        for dy in range(3):
            at = 18 + dy * 3 + dx
            value = jnp.where(band == dy, tiled[at : at + 1], value)
        w4_ref[dx * 8 : (dx + 1) * 8, :] = value


def put_rows(h_ref, at, value):
    rows = value.shape[0]
    h_ref[1, pl.ds(at, rows), :] = value.astype(BF16)
    h_ref[0, pl.ds(at, rows), :] = shifted(value, 1).astype(BF16)
    h_ref[2, pl.ds(at, rows), :] = shifted(value, -1).astype(BF16)


def clear_rows(h_ref, first, last, rows, width):
    for cond, start in ((first, 0), (last, rows - width)):

        @pl.when(cond)
        def _():
            h_ref[:, start * 16 : (start + width) * 16, :] = jnp.zeros((3, width * 16, PX), BF16)


def conv_layers(x_ref, xs_ref, w1_ref, w2_ref, w3_ref, w4_ref, ha_ref, hb_ref, first, last):
    for pol in range(2):
        value = x_ref[pol].astype(F32)
        base = pol * IMG_ROWS
        xs_ref[1, base : base + IMG_ROWS, :] = value.astype(BF16)
        xs_ref[0, base : base + IMG_ROWS, :] = shifted(value, 1).astype(BF16)
        xs_ref[2, base : base + IMG_ROWS, :] = shifted(value, -1).astype(BF16)
    for block in range(5):
        pieces = []
        for dx in range(3):
            for pol in range(2):
                at = pol * IMG_ROWS + block * 16
                pieces.append(xs_ref[dx, at : at + 32, :])
        value = dot(w1_ref[...], jnp.concatenate(pieces, 0))
        put_rows(ha_ref, block * 256, jnp.maximum(value, 0.0))
    clear_rows(ha_ref, first, last, 70, 3)
    hb_ref[:, 70 * 16 : 72 * 16, :] = jnp.zeros((3, 32, PX), BF16)
    for w_ref, src, dst, rows, width in (
        (w2_ref, ha_ref, hb_ref, 68, 2),
        (w3_ref, hb_ref, ha_ref, 66, 1),
    ):

        def block_body(block, carry):
            at = pl.multiple_of(block * 224, 32)
            value = dot(w_ref[0], src[0, pl.ds(at, 256), :])
            value = value + dot(w_ref[1], src[1, pl.ds(at, 256), :])
            value = value + dot(w_ref[2], src[2, pl.ds(at, 256), :])
            put_rows(dst, at, jnp.maximum(value, 0.0))
            return carry

        lax.fori_loop(0, 5, block_body, 0)
        clear_rows(dst, first, last, rows, width)


def last_layer(w4_ref, h_ref, logit_ref):
    for block in range(8):
        at = block * 128
        value = jnp.zeros((8, PX), F32)
        for dx in range(3):
            tap = w4_ref[dx * 8 : (dx + 1) * 8, 0:160].astype(BF16)
            value = value + dot(tap, h_ref[dx, at : at + 160, :])
        logit_ref[block * 8 : (block + 1) * 8, :] = value


def line_sums(value_ref, cell_ref, win_ref):
    cells = iota((128, PX), 0)
    quarter = iota((8, PX), 0)

    def pair(step, carry):
        parts, picks = [], []
        for k in range(2):
            line = step * 2 + k
            cell = cell_ref[pl.ds(line, 1), :]
            value = value_ref[pl.ds(line, 1), :]
            high = value.astype(BF16).astype(F32)
            picks.append(onehot(cells == cell % 128))
            here = quarter == cell // 128 + 4 * k
            parts.append(
                jnp.concatenate(
                    [jnp.where(here, high, 0.0), jnp.where(here, value - high, 0.0)], 0
                ).astype(BF16)
            )
        sums = dot(parts[0], picks[0], NT) + dot(parts[1], picks[1], NT)
        win_ref[pl.ds(pl.multiple_of(step * 8, 8), 8), :] = sums[0:8] + sums[8:16]
        return carry

    lax.fori_loop(0, AZ // 2, pair, 0)


def slot_rows(tile_ref, row_ref, pick_ref, mark_ref, devices):
    tile = tile_ref[...].astype(F32)
    line_s, line_l = iota((AZ, AZ), 0), iota((AZ, AZ), 1)
    tile_col = jnp.sum(jnp.where(line_s == line_l, tile, 0.0), 1, keepdims=True)
    same = (tile_col == tile) & (line_l < line_s)
    earlier = jnp.sum(jnp.where(same, 1.0, 0.0), 1, keepdims=True)
    row_col = jnp.sum(jnp.where(line_s == line_l, row_ref[...].astype(F32), 0.0), 1, keepdims=True)
    wide = (AZ, AZ * 4)
    mine = iota(wide, 1) // 4 == iota(wide, 0)
    code = jnp.sum(jnp.where(mine, tile_col * 8.0 + earlier * 4.0, 0.0), 0, keepdims=True)
    code = code + (iota((1, AZ * 4), 1) % 4).astype(F32)
    out = iota((devices * 8, AZ * 4), 0).astype(F32)
    pick_ref[...] = onehot(out == code)
    marks = jnp.where(iota((AZ * 4, AZ), 0) // 4 == iota((AZ * 4, AZ), 1), 1.0, 0.0).astype(BF16)
    spread = jnp.broadcast_to(row_col + 1.0, (AZ, 128)).astype(BF16)
    mark_ref[...] = dot(marks, spread).astype(BF16)


def device_kernel(devices, x_ref, ksmall_ref, k2_ref, k3_ref, geo_ref, cell_ref, tile_ref, row_ref,
                  frac_ref, send_ref, w1_ref, w2_ref, w3_ref, w4_ref, xs_ref, ha_ref, hb_ref,
                  logit_ref, win_ref, pick_ref, mark_ref):
    me = lax.axis_index("tx") * lax.axis_size("ty") + lax.axis_index("ty")
    build_weights(ksmall_ref, k2_ref, k3_ref, w1_ref, w2_ref, w3_ref, w4_ref)
    slot_rows(tile_ref, row_ref, pick_ref, mark_ref, devices)
    line_sums(geo_ref, cell_ref, win_ref)
    covered = jnp.concatenate([win_ref[...].astype(BF16), mark_ref[...]], 1)
    placed = dot(pick_ref[...], covered)
    send_ref[:, 8:16, :] = placed[:, 0:128].reshape(devices, 8, 128).astype(BF16)
    send_ref[:, 16:24, :] = placed[:, 128:256].reshape(devices, 8, 128).astype(BF16)
    conv_layers(x_ref, xs_ref, w1_ref, w2_ref, w3_ref, w4_ref, ha_ref, hb_ref,
                me == 0, me == devices - 1)
    last_layer(w4_ref, ha_ref, logit_ref)
    fraction = (1.0 / (1.0 + jnp.exp(-logit_ref[...]))).astype(BF16)
    frac_ref[...] = fraction
    logit_ref[...] = fraction.astype(F32) * geo_ref[...]
    line_sums(logit_ref, cell_ref, win_ref)
    placed = dot(pick_ref[...], win_ref[...].astype(BF16))
    send_ref[:, 0:8, :] = placed.reshape(devices, 8, 128).astype(BF16)


def build_placer(marks, placer_ref, devices):
    total = devices * 8
    row = iota((TILE, 128), 0).astype(F32)
    inner = iota((128, 128), 0)
    for chunk in range(total // 128):
        part = marks[chunk * 16 : (chunk + 1) * 16].astype(F32).reshape(128, 128)
        part = jnp.sum(jnp.where(inner == iota((128, 128), 1), part, 0.0), 0, keepdims=True)
        lane = iota((1, 128), 1)
        at = jnp.where(part > 0.5, part - 1.0 + ((lane // 2) % 2).astype(F32), -9.0)
        for half in range(2):
            hit = (row == at) & (lane % 2 == half)
            placer_ref[half * TILE : (half + 1) * TILE, chunk * 128 : (chunk + 1) * 128] = onehot(hit)


def tile_kernel(devices, got_ref, depth_ref, level_ref, placer_ref):
    build_placer(got_ref[:, 16:24, :], placer_ref, devices)
    parts = []
    for k in range(2):
        got = got_ref[:, k * 8 : (k + 1) * 8, :].astype(F32).reshape(devices * 8, 128).astype(BF16)
        parts.append(dot(placer_ref[...], got))
    for half in range(2):
        observed = parts[0][half * TILE : (half + 1) * TILE]
        covered = parts[1][half * TILE : (half + 1) * TILE]
        depth = depth_ref[:, half * 128 : (half + 1) * 128]
        wet = depth / (depth + WET_DEPTH)
        innovation = (observed - covered * wet) / (covered + 1.0)
        level_ref[:, half * 128 : (half + 1) * 128] = depth * jnp.exp(innovation)


def flow_steps(level_ref, conv_ref, rain_ref, dirs_ref, runoff_ref):
    def step(count, carry):
        for at in range(0, EXT_ROWS, 16):
            level = level_ref[at : at + 16, :]
            power = jnp.exp2(jnp.log2(jnp.abs(level)) * (2.0 / 3.0))
            runoff_ref[DEPTH + at : DEPTH + at + 16, :] = conv_ref[at : at + 16, :] * level * power
        runoff_ref[0:DEPTH, :] = runoff_ref[EXT_ROWS : EXT_ROWS + DEPTH, :]
        runoff_ref[EXT_ROWS + DEPTH :, :] = runoff_ref[DEPTH : 2 * DEPTH, :]
        for at in range(0, EXT_ROWS, 16):
            rows = [runoff_ref[DEPTH + at - dr : DEPTH + at - dr + 16, :] for dr in (-1, 0, 1)]
            dirs = [dirs_ref[k, at : at + 16, :] for k in range(3)]

            def take(k, code):
                return jnp.where(dirs[k] == code, rows[k], 0.0)

            left = take(0, 0) + take(1, 3) + take(2, 5)
            straight = take(0, 1) + take(2, 6)
            right = take(0, 2) + take(1, 4) + take(2, 7)
            gained = straight + pltpu.roll(right, 1, 1) + pltpu.roll(left, EXT_COLS - 1, 1)
            here = slice(at, at + 16)
            level_ref[here, :] = level_ref[here, :] + rain_ref[here, :] - rows[1] + gained
        return carry

    lax.fori_loop(0, SUBSTEPS, step, 0)


def flow_kernel(field_ref, out_ref, level_ref, conv_ref, rain_ref, dirs_ref, runoff_ref):
    level_ref[...] = field_ref[0]
    conv_ref[...] = RUNOFF_COEF * jnp.sqrt(field_ref[1])
    rain_ref[...] = field_ref[2]
    direction = field_ref[3].astype(I32)
    dirs_ref[0] = pltpu.roll(direction, EXT_ROWS - 1, 0)
    dirs_ref[1] = direction
    dirs_ref[2] = pltpu.roll(direction, 1, 0)
    flow_steps(level_ref, conv_ref, rain_ref, dirs_ref, runoff_ref)
    out_ref[...] = level_ref[...]


def shift_pair(x, axis, dim, width):
    size, length = lax.axis_size(axis), x.shape[dim]
    up = [(i, (i + 1) % size) for i in range(size - 1)]
    down = [(j, i) for i, j in up]
    before = lax.ppermute(lax.slice_in_dim(x, length - width, length, axis=dim), axis, up)
    after = lax.ppermute(lax.slice_in_dim(x, 0, width, axis=dim), axis, down)
    return before, after


def per_device(sar_image, kernel_first, kernel_second, kernel_third, kernel_last, geo_weight,
               cell_index, block_tile, block_row, depth, slope, flow_dir, rain):
    devices = lax.axis_size(("tx", "ty"))
    ksmall = jnp.concatenate(
        [
            kernel_first.transpose(2, 3, 1, 0).reshape(18, 16),
            kernel_last.transpose(0, 2, 3, 1).reshape(9, 16),
            jnp.zeros((5, 16), BF16),
        ],
        0,
    )
    k2 = kernel_second.transpose(2, 3, 0, 1).reshape(144, 16)
    k3 = kernel_third.transpose(2, 3, 0, 1).reshape(144, 16)
    before, after = shift_pair(sar_image, ("tx", "ty"), 1, HALO)
    image = jnp.concatenate(
        [before, sar_image, after, jnp.zeros((2, IMG_ROWS - AZ - 2 * HALO, PX), BF16)], 1
    )
    vmem = pl.BlockSpec(memory_space=pltpu.VMEM)
    fraction, send = pl.pallas_call(
        functools.partial(device_kernel, devices),
        name="swath",
        out_shape=(
            jax.ShapeDtypeStruct((AZ, PX), BF16),
            jax.ShapeDtypeStruct((devices, 24, 128), BF16),
        ),
        in_specs=[vmem] * 8,
        out_specs=(vmem, vmem),
        scratch_shapes=[
            pltpu.VMEM((256, 192), BF16),
            pltpu.VMEM((3, 224, 256), BF16),
            pltpu.VMEM((3, 224, 256), BF16),
            pltpu.VMEM((24, 256), F32),
            pltpu.VMEM((3, 2 * IMG_ROWS, PX), BF16),
            pltpu.VMEM((3, ROWS1 * 16, PX), BF16),
            pltpu.VMEM((3, ROWS1 * 16, PX), BF16),
            pltpu.VMEM((AZ, PX), F32),
            pltpu.VMEM((AZ * 4, 128), F32),
            pltpu.VMEM((devices * 8, AZ * 4), BF16),
            pltpu.VMEM((AZ * 4, 128), BF16),
        ],
    )(image, ksmall, k2, k3, geo_weight, cell_index, block_tile.reshape(1, AZ),
      block_row.reshape(1, AZ))
    got = lax.all_to_all(send, ("tx", "ty"), split_axis=0, concat_axis=0, tiled=True)
    level = pl.pallas_call(
        functools.partial(tile_kernel, devices),
        name="tile",
        out_shape=jax.ShapeDtypeStruct((TILE, TILE), F32),
        in_specs=[vmem] * 2,
        out_specs=vmem,
        scratch_shapes=[pltpu.VMEM((2 * TILE, devices * 8), BF16)],
    )(got, depth)
    fields = jnp.stack([level, slope, rain, flow_dir.astype(F32)])
    before, after = shift_pair(fields, "tx", 1, DEPTH)
    fields = jnp.concatenate([before, fields, after], 1)
    before, after = shift_pair(fields, "ty", 2, DEPTH)
    fill = jnp.zeros((4, EXT_ROWS, EXT_COLS - TILE - 2 * DEPTH), F32)
    fields = jnp.concatenate([before, fields, after, fill], 2)
    level = pl.pallas_call(
        flow_kernel,
        name="flow",
        out_shape=jax.ShapeDtypeStruct((EXT_ROWS, EXT_COLS), F32),
        in_specs=[vmem],
        out_specs=vmem,
        scratch_shapes=[
            pltpu.VMEM((EXT_ROWS, EXT_COLS), F32),
            pltpu.VMEM((EXT_ROWS, EXT_COLS), F32),
            pltpu.VMEM((EXT_ROWS, EXT_COLS), F32),
            pltpu.VMEM((3, EXT_ROWS, EXT_COLS), I32),
            pltpu.VMEM((EXT_ROWS + 2 * DEPTH, EXT_COLS), F32),
        ],
    )(fields)
    return fraction, level[DEPTH : DEPTH + TILE, DEPTH : DEPTH + TILE]


def solution(mesh):
    lines = P(("tx", "ty"), None)
    tiles = P("tx", "ty")
    return jax.shard_map(
        per_device,
        mesh=mesh,
        in_specs=(P(None, ("tx", "ty"), None), P(), P(), P(), P(), lines, lines, lines, lines,
                  tiles, tiles, tiles, tiles),
        out_specs=(lines, tiles),
        check_vma=False,
    )
```

```python
import functools

import jax
import jax.numpy as jnp
from jax import lax
from jax.experimental import pallas as pl
from jax.experimental.pallas import tpu as pltpu
from jax.sharding import PartitionSpec as P

F32 = jnp.float32
BF16 = jnp.bfloat16
I32 = jnp.int32

WIN_ROWS = 2
SUBSTEPS = 8
CAPACITY = 2
CHANNELS = 16
WET_DEPTH = 0.5
RUNOFF_COEF = 0.25

AZ = 64
PX = 512
HALO = 4
SIDE = 8
IMG_ROWS = 96
ROWS1 = 80
TILE = 256
DEPTH = 8
EXT_ROWS = TILE + 2 * DEPTH
EXT_COLS = TILE + 128
CORNERS = ((1, 1), (1, -1), (-1, 1), (-1, -1))

MESH = pl.DeviceIdType.MESH
NN = (((1,), (0,)), ((), ()))
NT = (((1,), (1,)), ((), ()))
TN = (((0,), (0,)), ((), ()))


def dot(a, b, dims=NN):
    return lax.dot_general(a, b, dims, preferred_element_type=F32)


def iota(shape, dim):
    return lax.broadcasted_iota(I32, shape, dim)


def onehot(cond):
    return jnp.where(cond, 1.0, 0.0).astype(BF16)


def shifted(x, step):
    width = x.shape[1]
    rolled = pltpu.roll(x, step % width, 1)
    edge = 0 if step == 1 else width - 1
    return jnp.where(iota(x.shape, 1) == edge, 0.0, rolled)


def build_weights(ksmall_ref, k2_ref, k3_ref, w1_ref, w2_ref, w3_ref, w4_ref):
    spread = onehot(iota((16, 256), 1) % 16 == iota((16, 256), 0))
    band = iota((16, 256), 1) // 16
    for k_ref, w_ref in ((k2_ref, w2_ref), (k3_ref, w3_ref)):
        tiled = dot(k_ref[...], spread)
        for dx in range(3):
            taps = [tiled[(dy * 3 + dx) * 16 : (dy * 3 + dx + 1) * 16] for dy in range(3)]
            for row in range(14):
                value = jnp.zeros((16, 256), F32)
                for dy in range(3):
                    value = jnp.where(band == row + dy, taps[dy], value)
                w_ref[dx, row * 16 : (row + 1) * 16, :] = value.astype(BF16)
    lane = iota((32, 192), 1)
    taps = []
    for dy in range(3):
        source = (dy * 3 + lane // 64) * 2 + (lane // 32) % 2
        taps.append(dot(ksmall_ref[...], onehot(iota((32, 192), 0) == source), TN))
    in_row = iota((16, 192), 1) % 32
    for row in range(16):
        value = jnp.zeros((16, 192), F32)
        for dy in range(3):
            value = jnp.where(in_row == row + dy + SIDE - HALO, taps[dy], value)
        w1_ref[row * 16 : (row + 1) * 16, :] = value.astype(BF16)
    tiled = dot(ksmall_ref[...], spread)
    band = iota((8, 256), 1) // 16 - iota((8, 256), 0)
    for dx in range(3):
        value = jnp.zeros((8, 256), F32)
        for dy in range(3):
            at = 18 + dy * 3 + dx
            value = jnp.where(band == dy, tiled[at : at + 1], value)
        w4_ref[dx * 8 : (dx + 1) * 8, :] = value


def put_rows(h_ref, at, value):
    rows = value.shape[0]
    h_ref[1, pl.ds(at, rows), :] = value.astype(BF16)
    h_ref[0, pl.ds(at, rows), :] = shifted(value, 1).astype(BF16)
    h_ref[2, pl.ds(at, rows), :] = shifted(value, -1).astype(BF16)


def clear_rows(h_ref, first, last, rows, width):
    for cond, start in ((first, 0), (last, rows - width)):

        @pl.when(cond)
        def _():
            h_ref[:, start * 16 : (start + width) * 16, :] = jnp.zeros((3, width * 16, PX), BF16)


def conv_layers(x_ref, side_ref, xs_ref, w1_ref, w2_ref, w3_ref, ha_ref, hb_ref, first, last):
    for pol in range(2):
        before = jnp.where(first, 0.0, side_ref[0, pol].astype(F32))
        after = jnp.where(last, 0.0, side_ref[1, pol].astype(F32))
        fill = jnp.zeros((IMG_ROWS - AZ - 2 * SIDE, PX), F32)
        value = jnp.concatenate([before, x_ref[pol].astype(F32), after, fill], 0)
        base = pol * IMG_ROWS
        xs_ref[1, base : base + IMG_ROWS, :] = value.astype(BF16)
        xs_ref[0, base : base + IMG_ROWS, :] = shifted(value, 1).astype(BF16)
        xs_ref[2, base : base + IMG_ROWS, :] = shifted(value, -1).astype(BF16)
    for block in range(5):
        pieces = []
        for dx in range(3):
            for pol in range(2):
                at = pol * IMG_ROWS + block * 16
                pieces.append(xs_ref[dx, at : at + 32, :])
        value = dot(w1_ref[...], jnp.concatenate(pieces, 0))
        put_rows(ha_ref, block * 256, jnp.maximum(value, 0.0))
    clear_rows(ha_ref, first, last, 70, 3)
    hb_ref[:, 70 * 16 : 72 * 16, :] = jnp.zeros((3, 32, PX), BF16)
    for w_ref, src, dst, rows, width in (
        (w2_ref, ha_ref, hb_ref, 68, 2),
        (w3_ref, hb_ref, ha_ref, 66, 1),
    ):

        def block_body(block, carry):
            at = pl.multiple_of(block * 224, 32)
            value = dot(w_ref[0], src[0, pl.ds(at, 256), :])
            value = value + dot(w_ref[1], src[1, pl.ds(at, 256), :])
            value = value + dot(w_ref[2], src[2, pl.ds(at, 256), :])
            put_rows(dst, at, jnp.maximum(value, 0.0))
            return carry

        lax.fori_loop(0, 5, block_body, 0)
        clear_rows(dst, first, last, rows, width)


def last_layer(w4_ref, h_ref, logit_ref):
    for block in range(8):
        at = block * 128
        value = jnp.zeros((8, PX), F32)
        for dx in range(3):
            tap = w4_ref[dx * 8 : (dx + 1) * 8, 0:160].astype(BF16)
            value = value + dot(tap, h_ref[dx, at : at + 160, :])
        logit_ref[block * 8 : (block + 1) * 8, :] = value


def line_sums(value_ref, cell_ref, win_ref):
    cells = iota((128, PX), 0)
    quarter = iota((8, PX), 0)

    def pair(step, carry):
        parts, picks = [], []
        for k in range(2):
            line = step * 2 + k
            cell = cell_ref[pl.ds(line, 1), :]
            value = value_ref[pl.ds(line, 1), :]
            high = value.astype(BF16).astype(F32)
            picks.append(onehot(cells == cell % 128))
            here = quarter == cell // 128 + 4 * k
            parts.append(
                jnp.concatenate(
                    [jnp.where(here, high, 0.0), jnp.where(here, value - high, 0.0)], 0
                ).astype(BF16)
            )
        sums = dot(parts[0], picks[0], NT) + dot(parts[1], picks[1], NT)
        win_ref[pl.ds(pl.multiple_of(step * 8, 8), 8), :] = sums[0:8] + sums[8:16]
        return carry

    lax.fori_loop(0, AZ // 2, pair, 0)


def slot_rows(tile_ref, row_ref, pick_ref, mark_ref, devices):
    tile = tile_ref[...].astype(F32)
    line_s, line_l = iota((AZ, AZ), 0), iota((AZ, AZ), 1)
    tile_col = jnp.sum(jnp.where(line_s == line_l, tile, 0.0), 1, keepdims=True)
    same = (tile_col == tile) & (line_l < line_s)
    earlier = jnp.sum(jnp.where(same, 1.0, 0.0), 1, keepdims=True)
    row_col = jnp.sum(jnp.where(line_s == line_l, row_ref[...].astype(F32), 0.0), 1, keepdims=True)
    wide = (AZ, AZ * 4)
    mine = iota(wide, 1) // 4 == iota(wide, 0)
    code = jnp.sum(jnp.where(mine, tile_col * 8.0 + earlier * 4.0, 0.0), 0, keepdims=True)
    code = code + (iota((1, AZ * 4), 1) % 4).astype(F32)
    out = iota((devices * 8, AZ * 4), 0).astype(F32)
    pick_ref[...] = onehot(out == code)
    marks = jnp.where(iota((AZ * 4, AZ), 0) // 4 == iota((AZ * 4, AZ), 1), 1.0, 0.0).astype(BF16)
    spread = jnp.broadcast_to(row_col + 1.0, (AZ, 128)).astype(BF16)
    mark_ref[...] = dot(marks, spread).astype(BF16)


def build_placer(marks, placer_ref, devices):
    total = devices * 8
    row = iota((TILE, 128), 0).astype(F32)
    inner = iota((128, 128), 0)
    for chunk in range(total // 128):
        part = marks[chunk * 16 : (chunk + 1) * 16].astype(F32).reshape(128, 128)
        part = jnp.sum(jnp.where(inner == iota((128, 128), 1), part, 0.0), 0, keepdims=True)
        lane = iota((1, 128), 1)
        at = jnp.where(part > 0.5, part - 1.0 + ((lane // 2) % 2).astype(F32), -9.0)
        for half in range(2):
            hit = (row == at) & (lane % 2 == half)
            placer_ref[half * TILE : (half + 1) * TILE, chunk * 128 : (chunk + 1) * 128] = onehot(hit)


def flow_steps(level_ref, conv_ref, rain_ref, dirs_ref, runoff_ref):
    def step(count, carry):
        for at in range(0, EXT_ROWS, 16):
            level = level_ref[at : at + 16, :]
            power = jnp.exp2(jnp.log2(jnp.abs(level)) * (2.0 / 3.0))
            runoff_ref[DEPTH + at : DEPTH + at + 16, :] = conv_ref[at : at + 16, :] * level * power
        runoff_ref[0:DEPTH, :] = runoff_ref[EXT_ROWS : EXT_ROWS + DEPTH, :]
        runoff_ref[EXT_ROWS + DEPTH :, :] = runoff_ref[DEPTH : 2 * DEPTH, :]
        for at in range(0, EXT_ROWS, 16):
            rows = [runoff_ref[DEPTH + at - dr : DEPTH + at - dr + 16, :] for dr in (-1, 0, 1)]
            dirs = [dirs_ref[k, at : at + 16, :] for k in range(3)]

            def take(k, code):
                return jnp.where(dirs[k] == code, rows[k], 0.0)

            left = take(0, 0) + take(1, 3) + take(2, 5)
            straight = take(0, 1) + take(2, 6)
            right = take(0, 2) + take(1, 4) + take(2, 7)
            gained = straight + pltpu.roll(right, 1, 1) + pltpu.roll(left, EXT_COLS - 1, 1)
            here = slice(at, at + 16)
            level_ref[here, :] = level_ref[here, :] + rain_ref[here, :] - rows[1] + gained
        return carry

    lax.fori_loop(0, SUBSTEPS, step, 0)


def covered_level(parts, depth_ref, level_ref):
    for half in range(2):
        lanes = slice(half * 128, (half + 1) * 128)
        observed = parts[0][half * TILE : (half + 1) * TILE]
        covered = parts[1][half * TILE : (half + 1) * TILE]
        depth = depth_ref[:, lanes]
        wet = depth / (depth + WET_DEPTH)
        innovation = (observed - covered * wet) / (covered + 1.0)
        level_ref[0:TILE, lanes] = depth * jnp.exp(innovation)


def pack_columns(block, low):
    lane = iota((16, 128), 1)
    packed = jnp.zeros((16, 128), F32)
    for group in range(16):
        moved = pltpu.roll(block[group * 16 : (group + 1) * 16], (group * 8 - low) % 128, 1)
        packed = jnp.where(lane // 8 == group, moved, packed)
    return packed


def unpack_columns(packed_left, packed_right, fill):
    lane = iota((16, 128), 1)
    out = []
    for group in range(16):
        right = pltpu.roll(packed_right, (-group * 8) % 128, 1)
        left = pltpu.roll(packed_left, (120 - group * 8) % 128, 1)
        out.append(jnp.where(lane < 8, right, jnp.where(lane >= 120, left, fill)))
    return jnp.concatenate(out, 0)


def fill_edges(field_ref, index, rows_ref, cols_ref, corners_ref):
    rows_ref[0, index] = field_ref[TILE - DEPTH : TILE, 0:TILE]
    rows_ref[1, index] = field_ref[0:DEPTH, 0:TILE]
    cols_ref[0, index] = pack_columns(field_ref[0:TILE, 128:256], 120)
    cols_ref[1, index] = pack_columns(field_ref[0:TILE, 0:128], 0)
    for k, (a, b) in enumerate(CORNERS):
        rows = slice(TILE - DEPTH, TILE) if a > 0 else slice(0, DEPTH)
        lanes = slice(128, 256) if b > 0 else slice(0, 128)
        corners_ref[k, index] = field_ref[rows, lanes]


def take_edges(field_ref, index, rows_ref, cols_ref, corners_ref, fill):
    lane = iota((DEPTH, 128), 1)
    field_ref[TILE : TILE + DEPTH, 0:TILE] = rows_ref[1, index]
    field_ref[TILE + DEPTH : EXT_ROWS, 0:TILE] = rows_ref[0, index]
    field_ref[0:TILE, TILE:EXT_COLS] = unpack_columns(cols_ref[0, index], cols_ref[1, index], fill)
    for at, down in ((TILE, -1), (TILE + DEPTH, 1)):
        left = corners_ref[CORNERS.index((down, 1)), index]
        right = corners_ref[CORNERS.index((down, -1)), index]
        both = jnp.where(lane < 8, right, jnp.where(lane >= 120, left, fill))
        field_ref[at : at + DEPTH, TILE:EXT_COLS] = both


def edge_copies(place, sent, got, send_sem, recv_sem):
    tx, ty, n_tx, n_ty = place
    steps = [((1, 0), 0, 0), ((-1, 0), 0, 1), ((0, 1), 1, 0), ((0, -1), 1, 1)]
    steps += [(step, 2, k) for k, step in enumerate(CORNERS)]
    copies = []
    for number, ((a, b), which, k) in enumerate(steps):
        copies.append(
            pltpu.make_async_remote_copy(
                src_ref=sent[which].at[k],
                dst_ref=got[which].at[k],
                send_sem=send_sem.at[number],
                recv_sem=recv_sem.at[number],
                device_id=(lax.rem(tx + a + n_tx, n_tx), lax.rem(ty + b + n_ty, n_ty)),
                device_id_type=MESH,
            )
        )
    return copies


def exchange(me, devices, n_ty, sent_ref, got_ref, own_sem, send_sem, recv_sem):
    own = pltpu.make_async_copy(sent_ref.at[me], got_ref.at[me], own_sem)
    own.start()

    def send(step, carry):
        peer = lax.rem(me + step, devices)
        pltpu.make_async_remote_copy(
            src_ref=sent_ref.at[peer],
            dst_ref=got_ref.at[me],
            send_sem=send_sem,
            recv_sem=recv_sem,
            device_id=(peer // n_ty, lax.rem(peer, n_ty)),
            device_id_type=MESH,
        ).start()
        return carry

    lax.fori_loop(1, devices, send, 0)
    return own


def wait_bytes(ref, count, sem):
    pltpu.make_async_copy(ref.at[pl.ds(0, count)], ref.at[pl.ds(0, count)], sem).wait()


def whole_kernel(n_tx, n_ty, *refs):
    (x_in, ksmall_ref, k2_ref, k3_ref, geo_in, cell_in, tile_ref, row_ref, depth_in, slope_in,
     dir_in, rain_in, frac_ref, out_ref,
     x_ref, geo_ref, cell_ref, depth_ref, dir_ref, slope_ref, rain_in_ref, in_sem,
     w1_ref, w2_ref, w3_ref, w4_ref, side_ref, xs_ref, ha_ref, hb_ref, logit_ref, win_ref,
     pick_ref, mark_ref, early_ref, early_got, late_ref, late_got, placer_ref,
     level_ref, conv_ref, rain_ref, dirs_ref, runoff_ref,
     rows_s, cols_s, corners_s, rows_g, cols_g, corners_g,
     rows_l, cols_l, corners_l, rows_m, cols_m, corners_m,
     side_send, side_recv, edge_send, edge_recv, last_send, last_recv,
     own_sem, early_send, early_recv, late_send, late_recv) = refs
    devices = n_tx * n_ty
    tx, ty = lax.axis_index("tx"), lax.axis_index("ty")
    me = tx * n_ty + ty
    place = (tx, ty, n_tx, n_ty)
    barrier = pltpu.get_barrier_semaphore()

    def greet(step, carry):
        peer = lax.rem(me + step, devices)
        pl.semaphore_signal(barrier, inc=1, device_id=(peer // n_ty, lax.rem(peer, n_ty)),
                            device_id_type=MESH)
        return carry

    lax.fori_loop(1, devices, greet, 0)
    loads = []
    for number, (src, dst) in enumerate(
        ((slope_in, slope_ref), (rain_in, rain_in_ref), (dir_in, dir_ref), (geo_in, geo_ref),
         (cell_in, cell_ref), (depth_in, depth_ref), (x_in, x_ref))
    ):
        loads.append(pltpu.make_async_copy(src, dst, in_sem.at[number]))
        loads[-1].start()
    build_weights(ksmall_ref, k2_ref, k3_ref, w1_ref, w2_ref, w3_ref, w4_ref)
    slot_rows(tile_ref, row_ref, pick_ref, mark_ref, devices)
    for load in loads:
        load.wait()
    conv_ref[0:TILE, 0:TILE] = RUNOFF_COEF * jnp.sqrt(slope_ref[...])
    rain_ref[0:TILE, 0:TILE] = rain_in_ref[...]
    dirs_ref[1, 0:TILE, 0:TILE] = dir_ref[...].astype(F32)
    direction = dirs_ref.at[1]
    for index, field in enumerate((conv_ref, rain_ref, direction)):
        fill_edges(field, index, rows_s, cols_s, corners_s)
    pl.semaphore_wait(barrier, devices - 1)

    sides = []
    for k, (step, at) in enumerate(((1, AZ - SIDE), (-1, 0))):
        peer = lax.rem(me + step + devices, devices)
        sides.append(
            pltpu.make_async_remote_copy(
                src_ref=x_ref.at[:, at : at + SIDE, :],
                dst_ref=side_ref.at[k],
                send_sem=side_send.at[k],
                recv_sem=side_recv.at[k],
                device_id=(peer // n_ty, lax.rem(peer, n_ty)),
                device_id_type=MESH,
            )
        )
        sides[-1].start()
    edges = edge_copies(place, (rows_s, cols_s, corners_s), (rows_g, cols_g, corners_g),
                        edge_send, edge_recv)
    for copy in edges:
        copy.start()
    line_sums(geo_ref, cell_ref, win_ref)
    covered = jnp.concatenate([win_ref[...].astype(BF16), mark_ref[...]], 1)
    placed = dot(pick_ref[...], covered)
    early_ref[:, 0:8, :] = placed[:, 0:128].reshape(devices, 8, 128).astype(BF16)
    early_ref[:, 8:16, :] = placed[:, 128:256].reshape(devices, 8, 128).astype(BF16)
    own_early = exchange(me, devices, n_ty, early_ref, early_got, own_sem.at[0], early_send, early_recv)

    for copy in sides:
        copy.wait()
    conv_layers(x_ref, side_ref, xs_ref, w1_ref, w2_ref, w3_ref, ha_ref, hb_ref,
                me == 0, me == devices - 1)
    last_layer(w4_ref, ha_ref, logit_ref)
    fraction = (1.0 / (1.0 + jnp.exp(-logit_ref[...]))).astype(BF16)
    frac_ref[...] = fraction
    logit_ref[...] = fraction.astype(F32) * geo_ref[...]
    line_sums(logit_ref, cell_ref, win_ref)
    placed = dot(pick_ref[...], win_ref[...].astype(BF16))
    late_ref[...] = placed.reshape(devices, 8, 128).astype(BF16)
    own_late = exchange(me, devices, n_ty, late_ref, late_got, own_sem.at[1], late_send, late_recv)

    for copy in edges:
        copy.wait()
    for index, (field, fill) in enumerate(((conv_ref, 0.0), (rain_ref, 0.0), (direction, 8.0))):
        take_edges(field, index, rows_g, cols_g, corners_g, fill)
    for cond, at in ((tx == n_tx - 1, TILE), (tx == 0, TILE + DEPTH)):

        @pl.when(cond)
        def _():
            conv_ref[at : at + DEPTH, :] = jnp.zeros((DEPTH, EXT_COLS), F32)

    lane = iota((EXT_ROWS, 128), 1)
    outside = ((ty == n_ty - 1) & (lane < 64)) | ((ty == 0) & (lane >= 64))
    conv_ref[:, TILE:EXT_COLS] = jnp.where(outside, 0.0, conv_ref[:, TILE:EXT_COLS])
    dirs_ref[0] = pltpu.roll(dirs_ref[1], EXT_ROWS - 1, 0)
    dirs_ref[2] = pltpu.roll(dirs_ref[1], 1, 0)
    own_early.wait()
    wait_bytes(early_got, devices - 1, early_recv)
    build_placer(early_got[:, 8:16, :], placer_ref, devices)
    parts = [None, None]
    got = early_got[:, 0:8, :].astype(F32).reshape(devices * 8, 128).astype(BF16)
    parts[1] = dot(placer_ref[...], got)
    own_late.wait()
    wait_bytes(late_got, devices - 1, late_recv)
    got = late_got[...].astype(F32).reshape(devices * 8, 128).astype(BF16)
    parts[0] = dot(placer_ref[...], got)
    covered_level(parts, depth_ref, level_ref)

    fill_edges(level_ref, 0, rows_l, cols_l, corners_l)
    lasts = edge_copies(place, (rows_l, cols_l, corners_l), (rows_m, cols_m, corners_m),
                        last_send, last_recv)
    for copy in lasts:
        copy.start()
    wait_bytes(early_ref, devices - 1, early_send)
    wait_bytes(late_ref, devices - 1, late_send)
    for copy in lasts:
        copy.wait()
    take_edges(level_ref, 0, rows_m, cols_m, corners_m, 0.0)
    flow_steps(level_ref, conv_ref, rain_ref, dirs_ref, runoff_ref)
    out_ref[...] = level_ref[0:TILE, 0:TILE]


def per_device(n_tx, n_ty, sar_image, kernel_first, kernel_second, kernel_third, kernel_last,
               geo_weight, cell_index, block_tile, block_row, depth, slope, flow_dir, rain):
    devices = n_tx * n_ty
    ksmall = jnp.concatenate(
        [
            kernel_first.transpose(2, 3, 1, 0).reshape(18, 16),
            kernel_last.transpose(0, 2, 3, 1).reshape(9, 16),
            jnp.zeros((5, 16), BF16),
        ],
        0,
    )
    k2 = kernel_second.transpose(2, 3, 0, 1).reshape(144, 16)
    k3 = kernel_third.transpose(2, 3, 0, 1).reshape(144, 16)
    vmem = pl.BlockSpec(memory_space=pltpu.VMEM)
    stay = pl.BlockSpec(memory_space=pl.ANY)
    dma = pltpu.SemaphoreType.DMA

    def edge_buffers(count):
        return [
            pltpu.VMEM((2, count, DEPTH, TILE), F32),
            pltpu.VMEM((2, count, 16, 128), F32),
            pltpu.VMEM((4, count, DEPTH, 128), F32),
        ]

    return pl.pallas_call(
        functools.partial(whole_kernel, n_tx, n_ty),
        name="assimilate",
        out_shape=(
            jax.ShapeDtypeStruct((AZ, PX), BF16),
            jax.ShapeDtypeStruct((TILE, TILE), F32),
        ),
        in_specs=[stay, vmem, vmem, vmem, stay, stay, vmem, vmem, stay, stay, stay, stay],
        out_specs=(vmem, vmem),
        scratch_shapes=[
            pltpu.VMEM((2, AZ, PX), BF16),
            pltpu.VMEM((AZ, PX), F32),
            pltpu.VMEM((AZ, PX), I32),
            pltpu.VMEM((TILE, TILE), F32),
            pltpu.VMEM((TILE, TILE), I32),
            pltpu.VMEM((TILE, TILE), F32),
            pltpu.VMEM((TILE, TILE), F32),
            dma((7,)),
            pltpu.VMEM((256, 192), BF16),
            pltpu.VMEM((3, 224, 256), BF16),
            pltpu.VMEM((3, 224, 256), BF16),
            pltpu.VMEM((24, 256), F32),
            pltpu.VMEM((2, 2, SIDE, PX), BF16),
            pltpu.VMEM((3, 2 * IMG_ROWS, PX), BF16),
            pltpu.VMEM((3, ROWS1 * 16, PX), BF16),
            pltpu.VMEM((3, ROWS1 * 16, PX), BF16),
            pltpu.VMEM((AZ, PX), F32),
            pltpu.VMEM((AZ * 4, 128), F32),
            pltpu.VMEM((devices * 8, AZ * 4), BF16),
            pltpu.VMEM((AZ * 4, 128), BF16),
            pltpu.VMEM((devices, 16, 128), BF16),
            pltpu.VMEM((devices, 16, 128), BF16),
            pltpu.VMEM((devices, 8, 128), BF16),
            pltpu.VMEM((devices, 8, 128), BF16),
            pltpu.VMEM((2 * TILE, devices * 8), BF16),
            pltpu.VMEM((EXT_ROWS, EXT_COLS), F32),
            pltpu.VMEM((EXT_ROWS, EXT_COLS), F32),
            pltpu.VMEM((EXT_ROWS, EXT_COLS), F32),
            pltpu.VMEM((3, EXT_ROWS, EXT_COLS), F32),
            pltpu.VMEM((EXT_ROWS + 2 * DEPTH, EXT_COLS), F32),
            *edge_buffers(3), *edge_buffers(3), *edge_buffers(1), *edge_buffers(1),
            dma((2,)), dma((2,)), dma((8,)), dma((8,)), dma((8,)), dma((8,)),
            dma((2,)), dma(()), dma(()), dma(()), dma(()),
        ],
        compiler_params=pltpu.CompilerParams(collective_id=0, has_side_effects=True),
    )(sar_image, ksmall, k2, k3, geo_weight, cell_index, block_tile.reshape(1, AZ),
      block_row.reshape(1, AZ), depth, slope, flow_dir, rain)


def solution(mesh):
    lines = P(("tx", "ty"), None)
    tiles = P("tx", "ty")
    return jax.shard_map(
        functools.partial(per_device, mesh.shape["tx"], mesh.shape["ty"]),
        mesh=mesh,
        in_specs=(P(None, ("tx", "ty"), None), P(), P(), P(), P(), lines, lines, lines, lines,
                  tiles, tiles, tiles, tiles),
        out_specs=(lines, tiles),
        check_vma=False,
    )
```

```python
import functools
import random

import jax
import jax.numpy as jnp
from jax import lax
from jax.experimental import pallas as pl
from jax.experimental.pallas import tpu as pltpu
from jax.sharding import PartitionSpec as P

F32 = jnp.float32
BF16 = jnp.bfloat16
I32 = jnp.int32

WIN_ROWS = 2
SUBSTEPS = 8
CAPACITY = 2
CHANNELS = 16
WET_DEPTH = 0.5
RUNOFF_COEF = 0.25

AZ = 64
PX = 512
HALO = 4
SIDE = 8
IMG_ROWS = 96
ROWS1 = 80
TILE = 256
DEPTH = 8
EXT_ROWS = TILE + 2 * DEPTH
EXT_COLS = TILE + 128
CORNERS = ((1, 1), (1, -1), (-1, 1), (-1, -1))

MESH = pl.DeviceIdType.MESH
LOGICAL = pl.DeviceIdType.LOGICAL
NN = (((1,), (0,)), ((), ()))
NT = (((1,), (1,)), ((), ()))
TN = (((0,), (0,)), ((), ()))


def dot(a, b, dims=NN):
    return lax.dot_general(a, b, dims, preferred_element_type=F32)


def iota(shape, dim):
    return lax.broadcasted_iota(I32, shape, dim)


def onehot(cond):
    return jnp.where(cond, 1.0, 0.0).astype(BF16)


def shifted(x, step):
    width = x.shape[1]
    rolled = pltpu.roll(x, step % width, 1)
    edge = 0 if step == 1 else width - 1
    return jnp.where(iota(x.shape, 1) == edge, 0.0, rolled)


def build_weights(ksmall_ref, k2_ref, k3_ref, w1_ref, w2_ref, w3_ref, w4_ref):
    spread = onehot(iota((16, 256), 1) % 16 == iota((16, 256), 0))
    band = iota((16, 256), 1) // 16
    for k_ref, w_ref in ((k2_ref, w2_ref), (k3_ref, w3_ref)):
        tiled = dot(k_ref[...], spread)
        for dx in range(3):
            taps = [tiled[(dy * 3 + dx) * 16 : (dy * 3 + dx + 1) * 16] for dy in range(3)]
            for row in range(14):
                value = jnp.zeros((16, 256), F32)
                for dy in range(3):
                    value = jnp.where(band == row + dy, taps[dy], value)
                w_ref[dx, row * 16 : (row + 1) * 16, :] = value.astype(BF16)
    lane = iota((32, 192), 1)
    taps = []
    for dy in range(3):
        source = (dy * 3 + lane // 64) * 2 + (lane // 32) % 2
        taps.append(dot(ksmall_ref[...], onehot(iota((32, 192), 0) == source), TN))
    in_row = iota((16, 192), 1) % 32
    for row in range(16):
        value = jnp.zeros((16, 192), F32)
        for dy in range(3):
            value = jnp.where(in_row == row + dy + SIDE - HALO, taps[dy], value)
        w1_ref[row * 16 : (row + 1) * 16, :] = value.astype(BF16)
    tiled = dot(ksmall_ref[...], spread)
    band = iota((8, 256), 1) // 16 - iota((8, 256), 0)
    for dx in range(3):
        value = jnp.zeros((8, 256), F32)
        for dy in range(3):
            at = 18 + dy * 3 + dx
            value = jnp.where(band == dy, tiled[at : at + 1], value)
        w4_ref[dx * 8 : (dx + 1) * 8, :] = value


def put_rows(h_ref, at, value):
    rows = value.shape[0]
    h_ref[1, pl.ds(at, rows), :] = value.astype(BF16)
    h_ref[0, pl.ds(at, rows), :] = shifted(value, 1).astype(BF16)
    h_ref[2, pl.ds(at, rows), :] = shifted(value, -1).astype(BF16)


def clear_rows(h_ref, first, last, rows, width):
    for cond, start in ((first, 0), (last, rows - width)):

        @pl.when(cond)
        def _():
            h_ref[:, start * 16 : (start + width) * 16, :] = jnp.zeros((3, width * 16, PX), BF16)


def image_rows(xs_ref, pol, at, value):
    base = pol * IMG_ROWS + at
    rows = value.shape[0]
    xs_ref[1, base : base + rows, :] = value
    xs_ref[0, base : base + rows, :] = shifted(value, 1)
    xs_ref[2, base : base + rows, :] = shifted(value, -1)


def first_block(block, xs_ref, w1_ref, ha_ref):
    pieces = []
    for dx in range(3):
        for pol in range(2):
            at = pol * IMG_ROWS + block * 16
            pieces.append(xs_ref[dx, at : at + 32, :].astype(BF16))
    value = dot(w1_ref[...], jnp.concatenate(pieces, 0))
    put_rows(ha_ref, block * 256, jnp.maximum(value, 0.0))


def wide_block(block, w_ref, src, dst):
    at = block * 224
    value = dot(w_ref[0], src[0, at : at + 256, :])
    value = value + dot(w_ref[1], src[1, at : at + 256, :])
    value = value + dot(w_ref[2], src[2, at : at + 256, :])
    put_rows(dst, at, jnp.maximum(value, 0.0))


def conv_inside(x_ref, xs_ref, w1_ref, w2_ref, ha_ref, hb_ref):
    for pol in range(2):
        image_rows(xs_ref, pol, SIDE, x_ref[pol].astype(F32))
        fill = IMG_ROWS - AZ - 2 * SIDE
        at = pol * IMG_ROWS + AZ + 2 * SIDE
        xs_ref[:, at : at + fill, :] = jnp.zeros((3, fill, PX), F32)
    for block in (1, 2, 3):
        first_block(block, xs_ref, w1_ref, ha_ref)
    for block in (2, 3):
        wide_block(block, w2_ref, ha_ref, hb_ref)


def conv_rest(side_ref, xs_ref, w1_ref, w2_ref, w3_ref, ha_ref, hb_ref, first, last):
    for pol in range(2):
        image_rows(xs_ref, pol, 0, jnp.where(first, 0.0, side_ref[0, pol].astype(F32)))
        image_rows(xs_ref, pol, SIDE + AZ, jnp.where(last, 0.0, side_ref[1, pol].astype(F32)))
    for block in (0, 4):
        first_block(block, xs_ref, w1_ref, ha_ref)
    clear_rows(ha_ref, first, last, 70, 3)
    hb_ref[:, 70 * 16 : 72 * 16, :] = jnp.zeros((3, 32, PX), BF16)
    for block in (0, 1, 4):
        wide_block(block, w2_ref, ha_ref, hb_ref)
    clear_rows(hb_ref, first, last, 68, 2)
    for block in range(5):
        wide_block(block, w3_ref, hb_ref, ha_ref)
    clear_rows(ha_ref, first, last, 66, 1)


def last_layer(w4_ref, h_ref, logit_ref):
    for block in range(8):
        at = block * 128
        value = jnp.zeros((8, PX), F32)
        for dx in range(3):
            tap = w4_ref[dx * 8 : (dx + 1) * 8, 0:160].astype(BF16)
            value = value + dot(tap, h_ref[dx, at : at + 160, :])
        logit_ref[block * 8 : (block + 1) * 8, :] = value


def line_sums(value_ref, cell_ref, win_ref):
    cells = iota((128, PX), 0)
    quarter = iota((8, PX), 0)

    def pair(step, carry):
        parts, picks = [], []
        for k in range(2):
            line = step * 2 + k
            cell = cell_ref[pl.ds(line, 1), :]
            value = value_ref[pl.ds(line, 1), :]
            high = value.astype(BF16).astype(F32)
            picks.append(onehot(cells == cell % 128))
            here = quarter == cell // 128 + 4 * k
            parts.append(
                jnp.concatenate(
                    [jnp.where(here, high, 0.0), jnp.where(here, value - high, 0.0)], 0
                ).astype(BF16)
            )
        sums = dot(parts[0], picks[0], NT) + dot(parts[1], picks[1], NT)
        win_ref[pl.ds(pl.multiple_of(step * 8, 8), 8), :] = sums[0:8] + sums[8:16]
        return carry

    lax.fori_loop(0, AZ // 2, pair, 0, unroll=8)


def slot_rows(tile_ref, row_ref, pick_ref, mark_ref, devices):
    tile = tile_ref[...].astype(F32)
    line_s, line_l = iota((AZ, AZ), 0), iota((AZ, AZ), 1)
    tile_col = jnp.sum(jnp.where(line_s == line_l, tile, 0.0), 1, keepdims=True)
    same = (tile_col == tile) & (line_l < line_s)
    earlier = jnp.sum(jnp.where(same, 1.0, 0.0), 1, keepdims=True)
    row_col = jnp.sum(jnp.where(line_s == line_l, row_ref[...].astype(F32), 0.0), 1, keepdims=True)
    wide = (AZ, AZ * 4)
    mine = iota(wide, 1) // 4 == iota(wide, 0)
    code = jnp.sum(jnp.where(mine, tile_col * 8.0 + earlier * 4.0, 0.0), 0, keepdims=True)
    code = code + (iota((1, AZ * 4), 1) % 4).astype(F32)
    out = iota((devices * 8, AZ * 4), 0).astype(F32)
    pick_ref[...] = onehot(out == code)
    marks = jnp.where(iota((AZ * 4, AZ), 0) // 4 == iota((AZ * 4, AZ), 1), 1.0, 0.0).astype(BF16)
    spread = jnp.broadcast_to(row_col + 1.0, (AZ, 128)).astype(BF16)
    mark_ref[...] = dot(marks, spread).astype(BF16)


def build_placer(marks, placer_ref, devices):
    total = devices * 8
    row = iota((TILE, 128), 0).astype(F32)
    inner = iota((128, 128), 0)
    for chunk in range(total // 128):
        part = marks[chunk * 16 : (chunk + 1) * 16].astype(F32).reshape(128, 128)
        part = jnp.sum(jnp.where(inner == iota((128, 128), 1), part, 0.0), 0, keepdims=True)
        lane = iota((1, 128), 1)
        at = jnp.where(part > 0.5, part - 1.0 + ((lane // 2) % 2).astype(F32), -9.0)
        for half in range(2):
            hit = (row == at) & (lane % 2 == half)
            placer_ref[half * TILE : (half + 1) * TILE, chunk * 128 : (chunk + 1) * 128] = onehot(hit)


def flow_steps(level_ref, conv_ref, rain_ref, dirs_ref, runoff_ref):
    def step(count, carry):
        for at in range(0, EXT_ROWS, 16):
            level = level_ref[at : at + 16, :]
            power = jnp.exp2(jnp.log2(jnp.abs(level)) * (2.0 / 3.0))
            runoff_ref[DEPTH + at : DEPTH + at + 16, :] = conv_ref[at : at + 16, :] * level * power
        runoff_ref[0:DEPTH, :] = runoff_ref[EXT_ROWS : EXT_ROWS + DEPTH, :]
        runoff_ref[EXT_ROWS + DEPTH :, :] = runoff_ref[DEPTH : 2 * DEPTH, :]
        for at in range(0, EXT_ROWS, 16):
            rows = [runoff_ref[DEPTH + at - dr : DEPTH + at - dr + 16, :] for dr in (-1, 0, 1)]
            dirs = [dirs_ref[k, at : at + 16, :] for k in range(3)]

            def take(k, code):
                return jnp.where(dirs[k] == code, rows[k], 0.0)

            left = take(0, 0) + take(1, 3) + take(2, 5)
            straight = take(0, 1) + take(2, 6)
            right = take(0, 2) + take(1, 4) + take(2, 7)
            gained = straight + pltpu.roll(right, 1, 1) + pltpu.roll(left, EXT_COLS - 1, 1)
            here = slice(at, at + 16)
            level_ref[here, :] = level_ref[here, :] + rain_ref[here, :] - rows[1] + gained
        return carry

    lax.fori_loop(0, SUBSTEPS, step, 0)


def covered_level(parts, depth_ref, level_ref):
    for half in range(2):
        lanes = slice(half * 128, (half + 1) * 128)
        observed = parts[0][half * TILE : (half + 1) * TILE]
        covered = parts[1][half * TILE : (half + 1) * TILE]
        depth = depth_ref[:, lanes]
        wet = depth / (depth + WET_DEPTH)
        innovation = (observed - covered * wet) / (covered + 1.0)
        level_ref[0:TILE, lanes] = depth * jnp.exp(innovation)


def pack_columns(block, low):
    lane = iota((16, 128), 1)
    packed = jnp.zeros((16, 128), F32)
    for group in range(16):
        moved = pltpu.roll(block[group * 16 : (group + 1) * 16], (group * 8 - low) % 128, 1)
        packed = jnp.where(lane // 8 == group, moved, packed)
    return packed


def unpack_columns(packed_left, packed_right, fill):
    lane = iota((16, 128), 1)
    out = []
    for group in range(16):
        right = pltpu.roll(packed_right, (-group * 8) % 128, 1)
        left = pltpu.roll(packed_left, (120 - group * 8) % 128, 1)
        out.append(jnp.where(lane < 8, right, jnp.where(lane >= 120, left, fill)))
    return jnp.concatenate(out, 0)


def fill_edges(field_ref, index, rows_ref, cols_ref, corners_ref):
    rows_ref[0, index] = field_ref[TILE - DEPTH : TILE, 0:TILE]
    rows_ref[1, index] = field_ref[0:DEPTH, 0:TILE]
    cols_ref[0, index] = pack_columns(field_ref[0:TILE, 128:256], 120)
    cols_ref[1, index] = pack_columns(field_ref[0:TILE, 0:128], 0)
    for k, (a, b) in enumerate(CORNERS):
        rows = slice(TILE - DEPTH, TILE) if a > 0 else slice(0, DEPTH)
        lanes = slice(128, 256) if b > 0 else slice(0, 128)
        corners_ref[k, index] = field_ref[rows, lanes]


def take_edges(field_ref, index, rows_ref, cols_ref, corners_ref, fill):
    lane = iota((DEPTH, 128), 1)
    field_ref[TILE : TILE + DEPTH, 0:TILE] = rows_ref[1, index]
    field_ref[TILE + DEPTH : EXT_ROWS, 0:TILE] = rows_ref[0, index]
    field_ref[0:TILE, TILE:EXT_COLS] = unpack_columns(cols_ref[0, index], cols_ref[1, index], fill)
    for at, down in ((TILE, -1), (TILE + DEPTH, 1)):
        left = corners_ref[CORNERS.index((down, 1)), index]
        right = corners_ref[CORNERS.index((down, -1)), index]
        both = jnp.where(lane < 8, right, jnp.where(lane >= 120, left, fill))
        field_ref[at : at + DEPTH, TILE:EXT_COLS] = both


def edge_copies(place, sent, got, send_sem, recv_sem):
    tx, ty, n_tx, n_ty = place
    steps = [((1, 0), 0, 0), ((-1, 0), 0, 1), ((0, 1), 1, 0), ((0, -1), 1, 1)]
    steps += [(step, 2, k) for k, step in enumerate(CORNERS)]
    copies = []
    for number, ((a, b), which, k) in enumerate(steps):
        copies.append(
            pltpu.make_async_remote_copy(
                src_ref=sent[which].at[k],
                dst_ref=got[which].at[k],
                send_sem=send_sem.at[number],
                recv_sem=recv_sem.at[number],
                device_id=(lax.rem(tx + a + n_tx, n_tx), lax.rem(ty + b + n_ty, n_ty)),
                device_id_type=MESH,
            )
        )
    return copies


def peers_of(tx, ty):
    z, x, y, core = lax.div(tx, 4), lax.rem(tx, 4), lax.div(ty, 2), lax.rem(ty, 2)
    zs = [lax.rem(z + step, 4) * 32 for step in range(4)]
    xs = [lax.rem(x + step, 4) * 8 for step in range(4)]
    ys = [lax.rem(y + step, 4) * 2 for step in range(4)]
    cores = [core, 1 - core]
    steps = [(a, b, c, d) for a in range(4) for b in range(4) for c in range(4) for d in range(2)]
    random.Random(3).shuffle(steps)
    steps.sort(key=lambda step: -sum(min(k, 4 - k) for k in step[:3]))
    return [zs[a] + xs[b] + ys[c] + cores[d] for a, b, c, d in steps if a or b or c or d]


def exchange(me, peers, sent_ref, got_ref, own_sem, send_sem, recv_sem):
    own = pltpu.make_async_copy(sent_ref.at[me], got_ref.at[me], own_sem)
    own.start()
    for peer in peers:
        pltpu.make_async_remote_copy(
            src_ref=sent_ref.at[peer],
            dst_ref=got_ref.at[me],
            send_sem=send_sem,
            recv_sem=recv_sem,
            device_id=peer,
            device_id_type=LOGICAL,
        ).start()
    return own


def wait_bytes(ref, count, sem):
    pltpu.make_async_copy(ref.at[pl.ds(0, count)], ref.at[pl.ds(0, count)], sem).wait()


def whole_kernel(n_tx, n_ty, *refs):
    (x_in, ksmall_ref, k2_ref, k3_ref, geo_in, cell_in, tile_ref, row_ref, depth_in, slope_in,
     dir_in, rain_in, frac_ref, out_ref,
     x_ref, geo_ref, cell_ref, depth_ref, dir_ref, slope_ref, rain_in_ref, in_sem,
     w1_ref, w2_ref, w3_ref, w4_ref, side_ref, xs_ref, ha_ref, hb_ref, logit_ref, win_ref,
     pick_ref, mark_ref, early_ref, early_got, late_ref, late_got, placer_ref,
     level_ref, conv_ref, rain_ref, dirs_ref, runoff_ref,
     rows_s, cols_s, corners_s, rows_g, cols_g, corners_g,
     rows_l, cols_l, corners_l, rows_m, cols_m, corners_m,
     side_send, side_recv, edge_send, edge_recv, last_send, last_recv,
     own_sem, early_send, early_recv, late_send, late_recv) = refs
    devices = n_tx * n_ty
    tx, ty = lax.axis_index("tx"), lax.axis_index("ty")
    me = tx * n_ty + ty
    place = (tx, ty, n_tx, n_ty)
    barrier = pltpu.get_barrier_semaphore()

    peers = peers_of(tx, ty)
    for peer in peers:
        pl.semaphore_signal(barrier, inc=1, device_id=peer, device_id_type=LOGICAL)
    loads = []
    for number, (src, dst) in enumerate(
        ((slope_in, slope_ref), (rain_in, rain_in_ref), (dir_in, dir_ref), (geo_in, geo_ref),
         (cell_in, cell_ref), (depth_in, depth_ref), (x_in, x_ref))
    ):
        loads.append(pltpu.make_async_copy(src, dst, in_sem.at[number]))
        loads[-1].start()
    build_weights(ksmall_ref, k2_ref, k3_ref, w1_ref, w2_ref, w3_ref, w4_ref)
    slot_rows(tile_ref, row_ref, pick_ref, mark_ref, devices)
    for load in loads:
        load.wait()
    conv_ref[0:TILE, 0:TILE] = RUNOFF_COEF * jnp.sqrt(slope_ref[...])
    rain_ref[0:TILE, 0:TILE] = rain_in_ref[...]
    dirs_ref[1, 0:TILE, 0:TILE] = dir_ref[...].astype(F32)
    direction = dirs_ref.at[1]
    for index, field in enumerate((conv_ref, rain_ref, direction)):
        fill_edges(field, index, rows_s, cols_s, corners_s)
    line_sums(geo_ref, cell_ref, win_ref)
    covered = jnp.concatenate([win_ref[...].astype(BF16), mark_ref[...]], 1)
    placed = dot(pick_ref[...], covered)
    early_ref[:, 0:8, :] = placed[:, 0:128].reshape(devices, 8, 128).astype(BF16)
    early_ref[:, 8:16, :] = placed[:, 128:256].reshape(devices, 8, 128).astype(BF16)
    pl.semaphore_wait(barrier, devices - 1)

    sides = []
    for k, (step, at) in enumerate(((1, AZ - SIDE), (-1, 0))):
        peer = lax.rem(me + step + devices, devices)
        sides.append(
            pltpu.make_async_remote_copy(
                src_ref=x_ref.at[:, at : at + SIDE, :],
                dst_ref=side_ref.at[k],
                send_sem=side_send.at[k],
                recv_sem=side_recv.at[k],
                device_id=(peer // n_ty, lax.rem(peer, n_ty)),
                device_id_type=MESH,
            )
        )
        sides[-1].start()
    edges = edge_copies(place, (rows_s, cols_s, corners_s), (rows_g, cols_g, corners_g),
                        edge_send, edge_recv)
    for copy in edges:
        copy.start()
    own_early = exchange(me, peers, early_ref, early_got, own_sem.at[0], early_send, early_recv)

    conv_inside(x_ref, xs_ref, w1_ref, w2_ref, ha_ref, hb_ref)
    for copy in sides:
        copy.wait()
    conv_rest(side_ref, xs_ref, w1_ref, w2_ref, w3_ref, ha_ref, hb_ref, me == 0, me == devices - 1)
    last_layer(w4_ref, ha_ref, logit_ref)
    fraction = (1.0 / (1.0 + jnp.exp(-logit_ref[...]))).astype(BF16)
    frac_ref[...] = fraction
    logit_ref[...] = fraction.astype(F32) * geo_ref[...]
    line_sums(logit_ref, cell_ref, win_ref)
    placed = dot(pick_ref[...], win_ref[...].astype(BF16))
    late_ref[...] = placed.reshape(devices, 8, 128).astype(BF16)
    own_late = exchange(me, peers, late_ref, late_got, own_sem.at[1], late_send, late_recv)

    for copy in edges:
        copy.wait()
    for index, (field, fill) in enumerate(((conv_ref, 0.0), (rain_ref, 0.0), (direction, 8.0))):
        take_edges(field, index, rows_g, cols_g, corners_g, fill)
    for cond, at in ((tx == n_tx - 1, TILE), (tx == 0, TILE + DEPTH)):

        @pl.when(cond)
        def _():
            conv_ref[at : at + DEPTH, :] = jnp.zeros((DEPTH, EXT_COLS), F32)

    lane = iota((EXT_ROWS, 128), 1)
    outside = ((ty == n_ty - 1) & (lane < 64)) | ((ty == 0) & (lane >= 64))
    conv_ref[:, TILE:EXT_COLS] = jnp.where(outside, 0.0, conv_ref[:, TILE:EXT_COLS])
    dirs_ref[0] = pltpu.roll(dirs_ref[1], EXT_ROWS - 1, 0)
    dirs_ref[2] = pltpu.roll(dirs_ref[1], 1, 0)
    own_early.wait()
    wait_bytes(early_got, devices - 1, early_recv)
    build_placer(early_got[:, 8:16, :], placer_ref, devices)
    parts = [None, None]
    got = early_got[:, 0:8, :].astype(F32).reshape(devices * 8, 128).astype(BF16)
    parts[1] = dot(placer_ref[...], got)
    own_late.wait()
    wait_bytes(late_got, devices - 1, late_recv)
    got = late_got[...].astype(F32).reshape(devices * 8, 128).astype(BF16)
    parts[0] = dot(placer_ref[...], got)
    covered_level(parts, depth_ref, level_ref)

    fill_edges(level_ref, 0, rows_l, cols_l, corners_l)
    lasts = edge_copies(place, (rows_l, cols_l, corners_l), (rows_m, cols_m, corners_m),
                        last_send, last_recv)
    for copy in lasts:
        copy.start()
    wait_bytes(early_ref, devices - 1, early_send)
    wait_bytes(late_ref, devices - 1, late_send)
    for copy in lasts:
        copy.wait()
    take_edges(level_ref, 0, rows_m, cols_m, corners_m, 0.0)
    flow_steps(level_ref, conv_ref, rain_ref, dirs_ref, runoff_ref)
    out_ref[...] = level_ref[0:TILE, 0:TILE]


def per_device(n_tx, n_ty, sar_image, kernel_first, kernel_second, kernel_third, kernel_last,
               geo_weight, cell_index, block_tile, block_row, depth, slope, flow_dir, rain):
    devices = n_tx * n_ty
    ksmall = jnp.concatenate(
        [
            kernel_first.transpose(2, 3, 1, 0).reshape(18, 16),
            kernel_last.transpose(0, 2, 3, 1).reshape(9, 16),
            jnp.zeros((5, 16), BF16),
        ],
        0,
    )
    k2 = kernel_second.transpose(2, 3, 0, 1).reshape(144, 16)
    k3 = kernel_third.transpose(2, 3, 0, 1).reshape(144, 16)
    vmem = pl.BlockSpec(memory_space=pltpu.VMEM)
    stay = pl.BlockSpec(memory_space=pl.ANY)
    dma = pltpu.SemaphoreType.DMA

    def edge_buffers(count):
        return [
            pltpu.VMEM((2, count, DEPTH, TILE), F32),
            pltpu.VMEM((2, count, 16, 128), F32),
            pltpu.VMEM((4, count, DEPTH, 128), F32),
        ]

    return pl.pallas_call(
        functools.partial(whole_kernel, n_tx, n_ty),
        name="assimilate",
        out_shape=(
            jax.ShapeDtypeStruct((AZ, PX), BF16),
            jax.ShapeDtypeStruct((TILE, TILE), F32),
        ),
        in_specs=[stay, vmem, vmem, vmem, stay, stay, vmem, vmem, stay, stay, stay, stay],
        out_specs=(vmem, vmem),
        scratch_shapes=[
            pltpu.VMEM((2, AZ, PX), BF16),
            pltpu.VMEM((AZ, PX), F32),
            pltpu.VMEM((AZ, PX), I32),
            pltpu.VMEM((TILE, TILE), F32),
            pltpu.VMEM((TILE, TILE), I32),
            pltpu.VMEM((TILE, TILE), F32),
            pltpu.VMEM((TILE, TILE), F32),
            dma((7,)),
            pltpu.VMEM((256, 192), BF16),
            pltpu.VMEM((3, 224, 256), BF16),
            pltpu.VMEM((3, 224, 256), BF16),
            pltpu.VMEM((24, 256), F32),
            pltpu.VMEM((2, 2, SIDE, PX), BF16),
            pltpu.VMEM((3, 2 * IMG_ROWS, PX), F32),
            pltpu.VMEM((3, ROWS1 * 16, PX), BF16),
            pltpu.VMEM((3, ROWS1 * 16, PX), BF16),
            pltpu.VMEM((AZ, PX), F32),
            pltpu.VMEM((AZ * 4, 128), F32),
            pltpu.VMEM((devices * 8, AZ * 4), BF16),
            pltpu.VMEM((AZ * 4, 128), BF16),
            pltpu.VMEM((devices, 16, 128), BF16),
            pltpu.VMEM((devices, 16, 128), BF16),
            pltpu.VMEM((devices, 8, 128), BF16),
            pltpu.VMEM((devices, 8, 128), BF16),
            pltpu.VMEM((2 * TILE, devices * 8), BF16),
            pltpu.VMEM((EXT_ROWS, EXT_COLS), F32),
            pltpu.VMEM((EXT_ROWS, EXT_COLS), F32),
            pltpu.VMEM((EXT_ROWS, EXT_COLS), F32),
            pltpu.VMEM((3, EXT_ROWS, EXT_COLS), F32),
            pltpu.VMEM((EXT_ROWS + 2 * DEPTH, EXT_COLS), F32),
            *edge_buffers(3), *edge_buffers(3), *edge_buffers(1), *edge_buffers(1),
            dma((2,)), dma((2,)), dma((8,)), dma((8,)), dma((8,)), dma((8,)),
            dma((2,)), dma(()), dma(()), dma(()), dma(()),
        ],
        compiler_params=pltpu.CompilerParams(collective_id=0, has_side_effects=True),
    )(sar_image, ksmall, k2, k3, geo_weight, cell_index, block_tile.reshape(1, AZ),
      block_row.reshape(1, AZ), depth, slope, flow_dir, rain)


def solution(mesh):
    lines = P(("tx", "ty"), None)
    tiles = P("tx", "ty")
    return jax.shard_map(
        functools.partial(per_device, mesh.shape["tx"], mesh.shape["ty"]),
        mesh=mesh,
        in_specs=(P(None, ("tx", "ty"), None), P(), P(), P(), P(), lines, lines, lines, lines,
                  tiles, tiles, tiles, tiles),
        out_specs=(lines, tiles),
        check_vma=False,
    )
```
